512 devices in a mesh: prow: 16 (over z_lo, x, core), pcol: 32 (over y, z_hi).
Axes of the slice: x: 4, y: 8, z: 8 (z_hi: 4, z_lo: 2; z = z_hi * 2 + z_lo), core: 2. Of those that a mesh axis runs over, the one named last changes fastest.
Arguments:
- matrix: float32 [6, 16, 128, 3, 32, 128], P(None, 'prow', None, None, 'pcol'), may hold values from -1 to 40, as said below
- row_codes: int32 [6, 16, 128], P(None, 'prow'), may hold values from 1 to 8
- col_codes: int32 [3, 32, 128], P(None, 'pcol'), may hold values from 1 to 8
- fault_tiles: int32 [96, 2], replicated, may hold values from 0 to 95, as said below
- fault_cells: int32 [96, 2], replicated, may hold values from 0 to 127
- fault_bits: int32 [96], replicated, may hold values from 1 to 2
Outputs:
- factored: float32 [6, 16, 128, 3, 32, 128], P(None, 'prow', None, None, 'pcol')
- col_check: float32 [3, 32, 128], P(None, 'pcol')
- row_check: float32 [6, 16, 128], P(None, 'prow')
- col_flags: float32 [3, 32], P(None, 'pcol')
- row_flags: float32 [6, 16], P(None, 'prow')
The draws below stay inside these ranges and needn't reach their ends.
Inputs may be any that keep to these rules, and one draw needn't show every extreme that they name: `matrix`: symmetric positive definite. `fault_tiles`: each tile row index appears in exactly one fault, and so does each tile column index.
All inputs are finite; a program needn't handle non-finite values.
Results may differ from the reference program's by a relative error of at most 0.0003.
Values sent between devices are 32-bit elements; how exact they have to be, the bound alone decides.
No kernel may reach another device: no remote copies, remote signals or barrier semaphores. Data moves between devices by JAX's collectives and lax.ppermute only.
A program may use at most 64 MiB of HBM per device.

```python
import math
import jax
import jax.numpy as jnp
from jax import lax

TILE = 128
ORDER = 12288
TILES = 96
STEPS = 2
FAULTS = 96
N_PROW = 16
N_PCOL = 32


def draw_matrix(key, part):
    spread_bound = 2.6 / math.sqrt(ORDER)
    perturb = jax.random.uniform(jax.random.fold_in(key, 11), (ORDER, ORDER), jnp.float32, -spread_bound, spread_bound)
    symmetric = (perturb + perturb.T) * 0.5
    diagonal_lift = jax.random.uniform(jax.random.fold_in(key, 12), (ORDER,), jnp.float32, 4.0, 8.0)
    diagonal_index = jnp.arange(ORDER, dtype=jnp.int32)
    symmetric = symmetric.at[diagonal_index, diagonal_index].add(diagonal_lift)
    return symmetric.reshape(TILES // N_PROW, N_PROW, TILE, TILES // N_PCOL, N_PCOL, TILE)


def draw_fault_tiles(key, part):
    fault_rows = jax.random.permutation(jax.random.fold_in(key, 21), TILES)
    fault_cols = jax.random.permutation(jax.random.fold_in(key, 22), TILES)
    return jnp.stack([fault_rows, fault_cols], axis=1).astype(jnp.int32)


def set_ends(result, key, least, top_value):
    longest = result.shape.index(max(result.shape))
    spots = []
    for shift in (0, 1):
        where = [jax.random.randint(jax.random.fold_in(key, axis), (), 0, length) for axis, length in enumerate(result.shape)]
        where[longest] = (where[longest] + shift) % result.shape[longest]
        spots.append(tuple(where))
    return result.at[spots[0]].set(least).at[spots[1]].set(top_value)


def setup_inputs(seed: int = 0) -> dict:
    splits = jax.random.split(jax.random.key(seed), 7)
    return {
        "matrix": draw_matrix(jax.random.fold_in(splits[6], 71), 0),
        "row_codes": set_ends(jax.random.randint(splits[1], (TILES // N_PROW, N_PROW, TILE), 1, 9), jax.random.fold_in(splits[1], 1), 1, 8).astype(jnp.int32),
        "col_codes": set_ends(jax.random.randint(splits[2], (TILES // N_PCOL, N_PCOL, TILE), 1, 9), jax.random.fold_in(splits[2], 1), 1, 8).astype(jnp.int32),
        "fault_tiles": draw_fault_tiles(jax.random.fold_in(splits[6], 71), 0),
        "fault_cells": set_ends(jax.random.randint(splits[4], (FAULTS, 2), 0, TILE), jax.random.fold_in(splits[4], 1), 0, TILE - 1).astype(jnp.int32),
        "fault_bits": set_ends(jax.random.randint(splits[5], (FAULTS,), 1, 3), jax.random.fold_in(splits[5], 1), 1, 2).astype(jnp.int32),
    }


precise = lax.Precision.HIGHEST

def reference(matrix, row_codes, col_codes, fault_tiles, fault_cells, fault_bits):
    whole_matrix = matrix.reshape(ORDER, ORDER)
    row_weights = row_codes.reshape(ORDER).astype(jnp.float32) * 0.25
    col_weights = col_codes.reshape(ORDER).astype(jnp.float32) * 0.25
    col_check = jnp.dot(row_weights, whole_matrix, precision=precise)
    row_check = jnp.dot(whole_matrix, col_weights, precision=precise)
    magnitude = jnp.exp2(fault_bits.astype(jnp.float32) - 1.0)
    fault_rows = (fault_tiles[:, 0] * TILE + fault_cells[:, 0]).astype(jnp.int32)
    fault_cols = (fault_tiles[:, 1] * TILE + fault_cells[:, 1]).astype(jnp.int32)
    whole_matrix = whole_matrix.at[fault_rows, fault_cols].add(magnitude)
    tile_index = jnp.arange(ORDER, dtype=jnp.int32) // TILE
    identity = jnp.eye(TILE, dtype=jnp.float32)
    for step_index in range(STEPS):
        first_row = step_index * TILE
        diagonal = whole_matrix[first_row:first_row + TILE, first_row:first_row + TILE]
        factor = jnp.linalg.cholesky(diagonal)
        inverse = jax.scipy.linalg.solve_triangular(factor, identity, lower=True)
        product = jnp.dot(whole_matrix[:, first_row:first_row + TILE], inverse.T, precision=precise)
        panel_cols = jnp.where((tile_index > step_index)[:, None], product, 0.0)
        panel_cols = panel_cols.at[first_row:first_row + TILE].set(factor)
        new_check = jnp.dot(inverse, col_check[first_row:first_row + TILE], precision=precise)
        shift_vector = jnp.dot(col_weights, panel_cols, precision=precise) - col_weights[first_row:first_row + TILE]
        row_check = row_check - jnp.dot(panel_cols, shift_vector, precision=precise)
        col_check = col_check - jnp.where(tile_index > step_index, jnp.dot(panel_cols, new_check, precision=precise), 0.0)
        col_check = col_check.at[first_row:first_row + TILE].set(new_check)
        trailing_panel = jnp.where((tile_index > step_index)[:, None], panel_cols, 0.0)
        whole_matrix = whole_matrix - jnp.dot(trailing_panel, trailing_panel.T, precision=precise)
        whole_matrix = whole_matrix.at[:, first_row:first_row + TILE].set(panel_cols)
        cleared = (tile_index == step_index)[:, None] & (tile_index > step_index)[None, :]
        whole_matrix = jnp.where(cleared, 0.0, whole_matrix)
    col_found = jnp.dot(row_weights, whole_matrix, precision=precise)
    row_found = jnp.dot(whole_matrix, col_weights, precision=precise)
    col_flags = jnp.max(jnp.abs(col_check - col_found).reshape(TILES, TILE), axis=1)
    row_flags = jnp.max(jnp.abs(row_check - row_found).reshape(TILES, TILE), axis=1)
    return (whole_matrix.reshape(matrix.shape), col_check.reshape(TILES // N_PCOL, N_PCOL, TILE), row_check.reshape(TILES // N_PROW, N_PROW, TILE), col_flags.reshape(TILES // N_PCOL, N_PCOL), row_flags.reshape(TILES // N_PROW, N_PROW))
```

```python
import jax
import jax.numpy as jnp
from jax import lax
from jax.sharding import PartitionSpec as P

precise = lax.Precision.HIGHEST


def spread(pieces, axis):
    return lax.all_to_all(pieces, axis, 0, 0, tiled=True)


def collect(piece, axis):
    count = lax.axis_size(axis)
    return spread(jnp.broadcast_to(piece[None], (count, *piece.shape)), axis)


def factor_tile(tile):
    factor = jnp.linalg.cholesky(tile)
    identity = jnp.eye(tile.shape[0], dtype=jnp.float32)
    inverse = jax.scipy.linalg.solve_triangular(factor, identity, lower=True)
    return factor, inverse


def local(matrix, row_codes, col_codes, fault_tiles, fault_cells, fault_bits):
    grid_rows = lax.axis_size("prow")
    grid_cols = lax.axis_size("pcol")
    grid_row = lax.axis_index("prow")
    grid_col = lax.axis_index("pcol")
    tile_rows, _, size, tile_cols, _, _ = matrix.shape
    rows = tile_rows * size
    cols = tile_cols * size
    blocks = matrix.reshape(rows, tile_cols, size)
    row_weights = row_codes.reshape(rows).astype(jnp.float32) * 0.25
    col_weights = col_codes.reshape(tile_cols, size).astype(jnp.float32) * 0.25
    tile_row = jnp.arange(tile_rows, dtype=jnp.int32) * grid_rows + grid_row
    tile_col = jnp.arange(tile_cols, dtype=jnp.int32) * grid_cols + grid_col
    offsets = jnp.arange(size, dtype=jnp.int32)
    own_rows = (tile_row[:, None] * size + offsets).reshape(rows)
    own_cols = (tile_col[:, None] * size + offsets).reshape(cols)

    part = size // grid_rows
    top = spread(blocks[:size].reshape(grid_rows, part * tile_cols, size), "prow")[:2]
    top = collect(top, "prow").reshape(grid_rows, 2, part, tile_cols, size)
    top = top.transpose(1, 0, 2, 3, 4).reshape(2, size, tile_cols, size)

    left = jnp.concatenate([blocks[:, 0, :], top[:, :, 0, :].reshape(2 * size, size)], axis=0)
    count = left.shape[0] // grid_cols
    left = spread(left.reshape(grid_cols, count, size), "pcol")[:2]
    left = collect(left, "pcol").transpose(1, 0, 2, 3).reshape(2, grid_cols * count, size)

    magnitude = jnp.exp2(fault_bits.astype(jnp.float32) - 1.0)
    fault_rows = fault_tiles[:, 0] * size + fault_cells[:, 0]
    fault_cols = fault_tiles[:, 1] * size + fault_cells[:, 1]
    lead = jnp.arange(2 * size, dtype=jnp.int32)

    def hits(marks, places):
        return (marks[:, None] == places[None, :]).astype(jnp.float32)

    panel_rows = jnp.concatenate([own_rows, lead, own_cols])
    hit_rows = hits(fault_rows, panel_rows) * magnitude[:, None]
    hit_lead = hits(fault_cols, lead)
    hit_cols = hits(fault_cols, own_cols)
    added = jnp.einsum("fr,fkc->krc", hit_rows, hit_lead.reshape(-1, 2, size), precision=precise)
    left_faulty = left + added[:, : rows + 2 * size]
    top_faulty = top.transpose(0, 2, 3, 1).reshape(2, cols, size) + added[:, rows + 2 * size :]

    factor0, inverse0 = factor_tile(left_faulty[0, rows : rows + size])
    below = jnp.einsum("ab,cb->ac", left_faulty[0, rows + size :], inverse0, precision=precise)
    square = left_faulty[1, rows + size :] - jnp.einsum("ab,cb->ac", below, below, precision=precise)
    factor1, inverse1 = factor_tile(square)

    panel = jnp.concatenate([left_faulty[:, :rows], top_faulty], axis=1)
    tile_of = jnp.concatenate([jnp.repeat(tile_row, size), jnp.repeat(tile_col, size)])[:, None]
    copies = tile_rows + tile_cols
    panel0 = jnp.einsum("ab,cb->ac", panel[0], inverse0, precision=precise)
    shifted = panel[1] - jnp.einsum("ab,cb->ac", panel0, below, precision=precise)
    panel1 = jnp.einsum("ab,cb->ac", shifted, inverse1, precision=precise)
    panel0 = jnp.where(tile_of > 0, panel0, jnp.tile(factor0, (copies, 1)))
    panel1 = jnp.where(tile_of > 1, panel1, jnp.where(tile_of == 1, jnp.tile(factor1, (copies, 1)), 0.0))
    trailing = jnp.concatenate(
        [jnp.where(tile_of > 0, panel0, 0.0), jnp.where(tile_of > 1, panel1, 0.0)], axis=1
    )
    update = jnp.einsum(
        "ab,jcb->ajc", trailing[:rows], trailing[rows:].reshape(tile_cols, size, 2 * size), precision=precise
    )
    faults_added = jnp.einsum("fr,fjc->rjc", hit_rows[:, :rows], hit_cols.reshape(-1, tile_cols, size), precision=precise)
    result = blocks + faults_added - update
    row_tile = tile_of[:rows, :, None]
    col_tile = tile_col[None, :, None]
    result = jnp.where(col_tile == 0, panel0[:rows, None, :], result)
    result = jnp.where(col_tile == 1, panel1[:rows, None, :], result)
    result = jnp.where((row_tile < 2) & (col_tile > row_tile), 0.0, result)

    col_clean = jnp.einsum("a,ajc->jc", row_weights, blocks, precision=precise)
    col_found = jnp.einsum("a,ajc->jc", row_weights, result, precision=precise)
    col_lead = jnp.einsum("a,kac->kc", row_weights, left[:, :rows], precision=precise)
    col_sums = jnp.concatenate([col_clean, col_found, col_lead])
    row_clean = jnp.einsum("ajc,jc->a", blocks, col_weights, precision=precise)
    row_found = jnp.einsum("ajc,jc->a", result, col_weights, precision=precise)
    flat_weights = col_weights.reshape(cols)
    steps = jnp.arange(2, dtype=jnp.int32)
    own_lead = jnp.where(steps[:, None] == grid_col, col_weights[0][None], 0.0)
    shift = jnp.stack(
        [
            jnp.einsum("a,ab->b", flat_weights, panel0[rows:], precision=precise),
            jnp.einsum("a,ab->b", flat_weights, panel1[rows:], precision=precise),
        ]
    )
    row_sums = jnp.concatenate(
        [row_clean.reshape(tile_rows, size), row_found.reshape(tile_rows, size), shift - own_lead]
    )
    col_sums = jnp.sum(collect(col_sums, "prow").reshape(grid_rows, *col_sums.shape), axis=0)
    row_sums = jnp.sum(collect(row_sums, "pcol").reshape(grid_cols, *row_sums.shape), axis=0)

    head0 = jnp.dot(inverse0, col_sums[2 * tile_cols], precision=precise)
    head1 = jnp.dot(
        inverse1, col_sums[2 * tile_cols + 1] - jnp.dot(below, head0, precision=precise), precision=precise
    )
    taken0 = jnp.dot(panel0[rows:], head0, precision=precise).reshape(tile_cols, size)
    taken1 = jnp.dot(panel1[rows:], head1, precision=precise).reshape(tile_cols, size)
    col_check = col_sums[:tile_cols] - taken0 - taken1
    col_check = jnp.where(tile_col[:, None] == 0, head0[None], col_check)
    col_check = jnp.where(tile_col[:, None] == 1, head1[None], col_check)
    row_taken = jnp.dot(panel0[:rows], row_sums[2 * tile_rows], precision=precise)
    row_taken = row_taken + jnp.dot(panel1[:rows], row_sums[2 * tile_rows + 1], precision=precise)
    row_check = row_sums[:tile_rows] - row_taken.reshape(tile_rows, size)
    col_flags = jnp.max(jnp.abs(col_check - col_sums[tile_cols : 2 * tile_cols]), axis=1)
    row_flags = jnp.max(jnp.abs(row_check - row_sums[tile_rows : 2 * tile_rows]), axis=1)
    return (
        result.reshape(matrix.shape),
        col_check.reshape(tile_cols, 1, size),
        row_check.reshape(tile_rows, 1, size),
        col_flags.reshape(tile_cols, 1),
        row_flags.reshape(tile_rows, 1),
    )


def solution(mesh):
    return jax.shard_map(
        local,
        mesh=mesh,
        in_specs=(
            P(None, "prow", None, None, "pcol", None),
            P(None, "prow", None),
            P(None, "pcol", None),
            P(),
            P(),
            P(),
        ),
        out_specs=(
            P(None, "prow", None, None, "pcol", None),
            P(None, "pcol", None),
            P(None, "prow", None),
            P(None, "pcol"),
            P(None, "prow"),
        ),
        check_vma=False,
    )
```
